512 devices in a mesh: dp: 4 (over x), expert: 8 (over y, core), tensor: 16 (over z).
Axes of the slice: x: 4, y: 4, z: 16, core: 2. Of those that a mesh axis runs over, the one named last changes fastest.
Arguments:
- tokens: bfloat16 [2048, 3072], P('expert', 'dp'), may hold values from -6 to 6
- route_ids: int32 [2048, 2], P('expert'), may hold values from 0 to 7, all different within a row; in each aligned block of 256 rows (0 to 255, 256 to 511, ...) at most 96 rows name the same one
- gates: float32 [2048, 2], P('expert'), may hold values from 0.2 to 1
- w_gate: bfloat16 [8, 3072, 8192], P('expert', 'dp', 'tensor'), may hold values from -0.109375 to 0.109375
- w_up: bfloat16 [8, 3072, 8192], P('expert', 'dp', 'tensor'), may hold values from -0.109375 to 0.109375
- w_down: bfloat16 [8, 8192, 3072], P('expert', 'tensor', 'dp'), may hold values from -0.0625 to 0.0625
Outputs:
- mixed: bfloat16 [2048, 3072], P('expert', 'dp')
The draws below stay inside these ranges and needn't reach their ends.
Inputs may be any that keep to these rules, and one draw needn't show every extreme that they name: `route_ids`: each token names two different experts. Among the 256 tokens of one index of expert, no expert is named by more than 96 tokens, a bound that some block reaches.
All inputs are finite; a program needn't handle non-finite values.
Results may differ from the reference program's by a relative error of at most 0.025.
Values may be sent and summed in bfloat16 or wider, within the bound.
A program may use at most 64 MiB of HBM per device.

```python
import math
import jax
import jax.numpy as jnp
import numpy as np
from jax import lax

D = 3072
FF = 8192
TOK_E = 256
EXPERTS = 8
TOKENS = 2048
CAP = 96
WIDTH_BLOCKS = 4


def level_of(key, shape, cuts, low, high):
    def one(axis_at, shards_of):
        heights = jax.random.uniform(jax.random.fold_in(jax.random.fold_in(key, 6), axis_at), (shards_of,), jnp.float32, low / len(cuts), high / len(cuts))
        return jnp.repeat(jnp.exp(heights), shape[axis_at] // shards_of).reshape((-1,) + (1,) * (len(shape) - axis_at - 1))

    gain = one(*cuts[0])
    for cut in cuts[1:]:
        gain = gain * one(*cut)
    return gain


def deal_out(stream_key, own, number, rows, amount, top, limit, lean):
    sequence = jax.random.permutation(stream_key, amount)
    crowded, common = load_shares(amount, rows * top, limit, lean, True), load_shares(amount, rows * top, limit, lean, False)
    places = jnp.arange(amount)

    def named(sizes, turn):
        used = int((sizes > 0).sum())
        fixed = max(1, used // 4)
        passed = fixed + (places - fixed + turn * (used - fixed)) % max(1, amount - fixed)
        return jnp.zeros((amount,), jnp.int32).at[sequence[jnp.where(places < fixed, places, passed)]].set(jnp.asarray(sizes, jnp.int32))

    sizes = jnp.where(number % 4 == 0, named(crowded, number // 4), named(common, number - number // 4 - 1))
    mixed = jax.random.permutation(jax.random.fold_in(own, 3), amount)
    source_of, receiver = mixed[0:amount // 2 * 2:2], mixed[1:amount // 2 * 2:2]
    margin = jnp.minimum(sizes[source_of] - 1, limit - sizes[receiver]) // 2
    margin = jnp.where((source_of == sequence[0]) | (receiver == sequence[0]) | (sizes[receiver] == 0), 0, jnp.maximum(margin, 0))
    passed = jax.random.randint(jax.random.fold_in(own, 4), (amount // 2,), 0, 1 << 20) % (margin + 1)
    sizes = sizes.at[source_of].add(-passed).at[receiver].add(passed)
    labels = jnp.searchsorted(jnp.cumsum(sizes), jnp.arange(rows * top), side="right").astype(jnp.int32)
    table = labels.reshape(top, rows).T
    table = table[jax.random.permutation(jax.random.fold_in(own, 1), rows)]
    turn = jax.random.randint(jax.random.fold_in(own, 2), (rows, 1), 0, top)
    return jnp.take_along_axis(table, (jnp.arange(top)[None, :] + turn) % top, axis=1)


def load_shares(amount, total, most, lean, full):
    weights = [(1 << 20) // math.isqrt(standing ** lean) + 1 for standing in range(1, amount + 1)]
    largest = most if full else min(most, max(-(-total // amount), total * weights[0] // sum(weights)))
    least = 1 if total - largest >= amount - 1 else 0
    counts, spare = [largest] + [least] * (amount - 1), total - largest - least * (amount - 1)
    while spare > 0:
        movable = [i for i in range(1, amount) if counts[i] < largest] or [i for i in range(1, amount) if counts[i] < most]
        pool, remaining = sum([weights[i] for i in movable]), spare
        for i in movable:
            addition = min(most - counts[i], max(1, remaining * weights[i] // pool), spare)
            counts[i] = counts[i] + addition
            spare = spare - addition
    return np.array(counts)


def bell_draw(key, dims, width, reach, cuts=(), kind=jnp.bfloat16):
    values = width * jax.random.normal(key, dims, jnp.float32)
    if cuts:
        values = values * level_of(key, dims, cuts, -0.22, 0.18)
    return jnp.clip(values, -reach, reach).astype(kind)


def setup_inputs(seed: int = 0) -> dict:
    key_list = jax.random.split(jax.random.key(seed), 7)
    tokens = bell_draw(key_list[0], (TOKENS, D), 1.0, 6.0, ((0, 8), (1, 4)))
    route_ids_keys = jax.random.split(jax.random.fold_in(key_list[1], 1), TOKENS // TOK_E)
    route_ids_turns = jax.random.permutation(jax.random.fold_in(key_list[1], 3), TOKENS // TOK_E)
    route_ids = jax.vmap(lambda own, number: deal_out(jax.random.fold_in(key_list[1], 2), own, number, TOK_E, EXPERTS, 2, CAP, 2))(route_ids_keys, route_ids_turns).reshape((TOKENS, 2))
    gates = jnp.clip(0.2 + 0.8 * jax.random.uniform(key_list[2], (TOKENS, 2), jnp.float32) ** level_of(key_list[2], (TOKENS, 2), ((0, 8),), -0.2, 0.2), 0.2, 1.0)
    w_gate = bell_draw(key_list[3], (EXPERTS, D, FF), D ** -0.5, 0.109375, ((0, 8), (1, 4), (2, 16)))
    w_up = bell_draw(key_list[4], (EXPERTS, D, FF), D ** -0.5, 0.109375, ((0, 8), (1, 4), (2, 16)))
    w_down = bell_draw(key_list[5], (EXPERTS, FF, D), FF ** -0.5, 0.0625, ((0, 8), (1, 16), (2, 4)))
    return dict(tokens=tokens, route_ids=route_ids, gates=gates, w_gate=w_gate, w_up=w_up, w_down=w_down)


def slot_index(route_group):
    flat = route_group.reshape(-1)
    hits = (flat[:, None] == jnp.arange(EXPERTS, dtype=jnp.int32)[None, :]).astype(jnp.int32)
    before = jnp.cumsum(hits, axis=0) - hits
    rank = jnp.sum(before * hits, axis=1)
    return (rank * EXPERTS + flat).reshape(-1, 2).astype(jnp.int32)


def reference(tokens, route_ids, gates, w_gate, w_up, w_down):
    groups = tokens.reshape(EXPERTS, TOK_E, D)
    where = jax.vmap(slot_index)(route_ids.reshape(EXPERTS, TOK_E, 2))

    def fill(rows, place):
        buffer = jnp.zeros((CAP * EXPERTS, D), jnp.bfloat16)
        return buffer.at[place.reshape(-1)].set(jnp.repeat(rows, 2, axis=0))

    sent = jax.vmap(fill)(groups, where).reshape(EXPERTS, CAP, EXPERTS, D)
    block_width = D // WIDTH_BLOCKS

    def run_expert(number):
        rows = sent[:, :, number, :].transpose(1, 0, 2).reshape(CAP * EXPERTS, D).astype(jnp.float32)
        wg = w_gate[number].astype(jnp.float32)
        wu = w_up[number].astype(jnp.float32)
        gate = jnp.zeros((CAP * EXPERTS, FF), jnp.float32)
        up_sum = jnp.zeros((CAP * EXPERTS, FF), jnp.float32)
        for block in range(WIDTH_BLOCKS):
            lower = block * block_width
            part = rows[:, lower:lower + block_width]
            g_part = jnp.dot(part, wg[lower:lower + block_width], preferred_element_type=jnp.float32)
            u_part = jnp.dot(part, wu[lower:lower + block_width], preferred_element_type=jnp.float32)
            g_part, u_part = lax.optimization_barrier((g_part.astype(jnp.bfloat16), u_part.astype(jnp.bfloat16)))
            gate = gate + g_part.astype(jnp.float32)
            up_sum = up_sum + u_part.astype(jnp.float32)
        hidden = (jax.nn.silu(gate) * up_sum).astype(jnp.bfloat16)
        result = jnp.dot(hidden.astype(jnp.float32), w_down[number].astype(jnp.float32), preferred_element_type=jnp.float32)
        return result.astype(jnp.bfloat16).reshape(CAP, EXPERTS, D)

    done = lax.map(run_expert, jnp.arange(EXPERTS, dtype=jnp.int32))
    table = done.transpose(2, 1, 0, 3).reshape(EXPERTS, CAP * EXPERTS, D)

    def combine(rows_table, place, weights):
        first = rows_table[place[:, 0]].astype(jnp.float32)
        second = rows_table[place[:, 1]].astype(jnp.float32)
        return (weights[:, 0:1] * first + weights[:, 1:2] * second).astype(jnp.bfloat16)

    mixed = jax.vmap(combine)(table, where, gates.reshape(EXPERTS, TOK_E, 2))
    return mixed.reshape(TOKENS, D)
```

```python
import jax
import jax.numpy as jnp
from jax import lax
from jax.experimental import pallas as pl
from jax.experimental.pallas import tpu as pltpu
from jax.sharding import PartitionSpec as P

BF = jnp.bfloat16
F32 = jnp.float32
RING = 4
CAP = 96
ROWS = 2 * CAP
PART = ROWS // RING
NONE = -1000.0
NSEM = 110


def kernel(tok, route, gates, wg_h, wu_h, wd_h, out, *s):
    (wg, wu, wd, slots, pick, rows, dhop, part, rl, fin, cmb, hid, obuf, rhop, ret, gm, acc,
     zs, zrl, zfin, zcmb, ys, yrl, yfin, ycmb, zo, wsem, ssem, rsem, barrier_unused) = s
    width = tok.shape[1]
    tokens = tok.shape[0]
    x = lax.axis_index("dp")
    e = lax.axis_index("expert")
    z = lax.axis_index("tensor")
    y, c = lax.div(e, 2), lax.rem(e, 2)
    nz = RING * RING

    def chip(j):
        return lax.rem(y + j, RING)

    def dev_e(j, core):
        return {"expert": chip(j) * 2 + core}

    def dev_x(j):
        return {"dp": lax.rem(x + j, RING)}

    def dev_z(j):
        return {"tensor": lax.rem(z + nz + j, nz)}

    loads = [pltpu.make_async_copy(a, b, wsem.at[i])
             for i, (a, b) in enumerate(((wg_h, wg), (wu_h, wu), (wd_h, wd)))]
    for load in loads:
        load.start()

    barrier = pltpu.get_barrier_semaphore()
    peers = [dev_e(0, 1 - c)] + [dev_e(j, k) for j in (1, 3) for k in (0, 1)]
    peers += [dev_x(1), dev_x(3)] + [dev_z(j) for j in (1, -1, 4, -4)]
    for peer in peers:
        pl.semaphore_signal(barrier, inc=1, device_id=peer, device_id_type=pl.DeviceIdType.MESH)

    used = [0]
    pending = []

    def take(n=1):
        used[0] += n
        assert used[0] <= NSEM
        return used[0] - n

    def send(src, dst, dev, k, k_recv):
        copy = pltpu.make_async_remote_copy(
            src_ref=src, dst_ref=dst, send_sem=ssem.at[k], recv_sem=rsem.at[k_recv],
            device_id=dev, device_id_type=pl.DeviceIdType.MESH)
        copy.start()
        pending.append(copy)
        return copy

    def arrived(dst, k):
        pltpu.make_async_remote_copy(
            src_ref=dst, dst_ref=dst, send_sem=ssem.at[0], recv_sem=rsem.at[k],
            device_id=dev_e(0, 1 - c), device_id_type=pl.DeviceIdType.MESH).wait_recv()

    r0, r1 = route[:, 0:1], route[:, 1:2]
    lane = lax.broadcasted_iota(jnp.int32, (tokens, 128), 1)
    hit0, hit1 = lane == r0, lane == r1
    hits = jnp.where(hit0 | hit1, 1.0, 0.0)
    earlier = jnp.where(
        lax.broadcasted_iota(jnp.int32, (tokens, tokens), 1)
        < lax.broadcasted_iota(jnp.int32, (tokens, tokens), 0), 1.0, 0.0)
    rank = jnp.dot(earlier.astype(BF), hits.astype(BF), preferred_element_type=F32)
    slots[...] = jnp.where(hit0 | hit1, rank, NONE).T

    def picked(j):
        line = lax.broadcasted_iota(jnp.int32, (ROWS, tokens), 0).astype(F32)
        first = slots[pl.ds(chip(j) * 2, 1), :]
        second = slots[pl.ds(chip(j) * 2 + 1, 1), :] + float(CAP)
        chosen = jnp.where((line == first) | (line == second), 1.0, 0.0).astype(BF)
        got = jnp.dot(chosen, tok[...], preferred_element_type=F32).astype(BF)
        pick[j] = got.reshape(2, CAP, width)

    half = CAP // 2
    ks_d = {j: take(2) for j in (1, 3)}
    k_dhop = take(2)
    k_fwd = {1: take(2), 3: take(2)}
    k_own = take()

    picked(2)
    pl.semaphore_wait(barrier, len(peers))
    send(pick.at[2, :, 0:half], dhop.at[0], dev_e(1, c), k_dhop, k_dhop)
    send(pick.at[2, :, half:CAP], dhop.at[1], dev_e(3, c), k_dhop + 1, k_dhop + 1)
    for j in (1, 3):
        picked(j)
        for core in (0, 1):
            send(pick.at[j, core], rows.at[RING - j, c], dev_e(j, core), ks_d[j] + core, ks_d[j] + c)
    picked(0)
    send(pick.at[0, 1 - c], rows.at[0, c], dev_e(0, 1 - c), k_own, k_own)
    rows[0, c] = pick[0, c]

    def dispatch_forward():
        arrived(dhop.at[0], k_dhop)
        for core in (0, 1):
            send(dhop.at[0, core], rows.at[2, c, 0:half], dev_e(1, core), k_fwd[1] + core, k_fwd[1] + c)
        arrived(dhop.at[1], k_dhop + 1)
        for core in (0, 1):
            send(dhop.at[1, core], rows.at[2, c, half:CAP], dev_e(3, core), k_fwd[3] + core, k_fwd[3] + c)

    def rows_here(j):
        if j == 0:
            arrived(rows.at[0, 1 - c], k_own)
        elif j == 2:
            for core in (0, 1):
                arrived(rows.at[2, core, 0:half], k_fwd[1] + core)
                arrived(rows.at[2, core, half:CAP], k_fwd[3] + core)
        else:
            for core in (0, 1):
                arrived(rows.at[j, core], ks_d[RING - j] + core)

    def rs_start(own, i, left, right, relay, done):
        k = take(6)
        opp, r, l = lax.rem(i + 2, RING), lax.rem(i + 1, RING), lax.rem(i + 3, RING)
        send(own.at[0, opp], relay.at[0], right, k, k)
        send(own.at[1, opp], relay.at[1], left, k + 1, k + 1)
        send(own.at[1, r], done.at[0], right, k + 2, k + 2)
        send(own.at[0, l], done.at[1], left, k + 3, k + 3)
        return k

    def rs_relay(k, own, i, left, right, relay, done, mixed):
        r, l = lax.rem(i + 1, RING), lax.rem(i + 3, RING)
        arrived(relay.at[0], k)
        mixed[0] = (own[0, r].astype(F32) + relay[0].astype(F32)).astype(BF)
        send(mixed.at[0], done.at[2], right, k + 4, k + 4)
        arrived(relay.at[1], k + 1)
        mixed[1] = (own[1, l].astype(F32) + relay[1].astype(F32)).astype(BF)
        send(mixed.at[1], done.at[3], left, k + 5, k + 5)

    def rs_finish(k, own, i, done):
        for n in range(4):
            arrived(done.at[n], k + 2 + n)
        first = own[0, i].astype(F32) + done[1].astype(F32) + done[2].astype(F32)
        second = own[1, i].astype(F32) + done[0].astype(F32) + done[3].astype(F32)
        return first, second

    def ag_start(at, i, left, right):
        k = take(6)
        send(at(0, i), at(0, i), right, k, k)
        send(at(1, i), at(1, i), left, k + 1, k + 1)
        send(at(1, i), at(1, i), right, k + 2, k + 2)
        send(at(0, i), at(0, i), left, k + 3, k + 3)
        return k

    def ag_relay(k, at, i, left, right):
        r, l = lax.rem(i + 1, RING), lax.rem(i + 3, RING)
        arrived(at(0, l), k)
        send(at(0, l), at(0, l), right, k + 4, k + 4)
        arrived(at(1, r), k + 1)
        send(at(1, r), at(1, r), left, k + 5, k + 5)

    def ag_finish(k, at, i):
        opp, r, l = lax.rem(i + 2, RING), lax.rem(i + 1, RING), lax.rem(i + 3, RING)
        arrived(at(1, l), k + 2)
        arrived(at(0, r), k + 3)
        arrived(at(0, opp), k + 4)
        arrived(at(1, opp), k + 5)

    xl, xr = dev_x(3), dev_x(1)
    rs_k, ag_k = {}, {}

    def hid_at(j):
        return lambda h, i: hid.at[j, h, i]

    def G(j):
        rows_here(j)
        if j == 0:
            loads[0].wait()
            loads[1].wait()
        here = rows[j].reshape(ROWS, width)
        for n, w in enumerate((wg, wu)):
            got = jnp.dot(here, w[...], preferred_element_type=F32).astype(BF)
            part[j, n] = got.reshape(RING, PART, got.shape[1])
        rs_k[j] = rs_start(part.at[j], x, xl, xr, rl.at[j], fin.at[j])

    def R(j):
        rs_relay(rs_k[j], part.at[j], x, xl, xr, rl.at[j], fin.at[j], cmb.at[j])

    def H(j):
        gate, up = rs_finish(rs_k[j], part.at[j], x, fin.at[j])
        got = (gate / (1.0 + jnp.exp(-gate)) * up).astype(BF)
        hw = got.shape[1] // 2
        hid[j, 0, x] = got[:, :hw]
        hid[j, 1, x] = got[:, hw:]
        ag_k[j] = ag_start(hid_at(j), x, xl, xr)

    def F(j):
        ag_relay(ag_k[j], hid_at(j), x, xl, xr)

    k_ret = {j: take(2) for j in (1, 3)}
    k_rhop = take(2)
    k_rfwd = {1: take(2), 3: take(2)}
    k_rown = take()

    def O(j, first_use=False):
        ag_finish(ag_k[j], hid_at(j), x)
        if first_use:
            loads[2].wait()
        hw = wd.shape[0] // 2
        got = jnp.dot(hid[j, 0].reshape(ROWS, hw), wd[0:hw], preferred_element_type=F32)
        got += jnp.dot(hid[j, 1].reshape(ROWS, hw), wd[hw:], preferred_element_type=F32)
        obuf[j] = got.astype(BF).reshape(2, CAP, width)
        if j == 0:
            send(obuf.at[0, 1 - c], ret.at[0, c], dev_e(0, 1 - c), k_rown, k_rown)
            ret[0, c] = obuf[0, c]
        elif j == 2:
            send(obuf.at[2, :, 0:half], rhop.at[0], dev_e(1, c), k_rhop, k_rhop)
            send(obuf.at[2, :, half:CAP], rhop.at[1], dev_e(3, c), k_rhop + 1, k_rhop + 1)
        else:
            for core in (0, 1):
                send(obuf.at[j, core], ret.at[RING - j, c], dev_e(j, core), k_ret[j] + core, k_ret[j] + c)

    def return_forward():
        arrived(rhop.at[0], k_rhop)
        for core in (0, 1):
            send(rhop.at[0, core], ret.at[2, c, 0:half], dev_e(1, core), k_rfwd[1] + core, k_rfwd[1] + c)
        arrived(rhop.at[1], k_rhop + 1)
        for core in (0, 1):
            send(rhop.at[1, core], ret.at[2, c, half:CAP], dev_e(3, core), k_rfwd[3] + core, k_rfwd[3] + c)

    def combine_table():
        ranks = jnp.where(hit0, rank, 0.0), jnp.where(hit1, rank, 0.0)
        places = [jnp.sum(v, axis=1, keepdims=True) + r.astype(F32) * float(CAP)
                  for v, r in zip(ranks, (r0, r1))]
        column = lax.broadcasted_iota(jnp.int32, (tokens, ROWS), 1)
        for j in range(RING):
            here = (column + chip(j) * ROWS).astype(F32)
            weight = jnp.where(here == places[0], gates[:, 0:1], 0.0)
            weight += jnp.where(here == places[1], gates[:, 1:2], 0.0)
            gm[j] = weight.astype(BF)

    def C(j, first=False):
        if j == 0:
            arrived(ret.at[0, 1 - c], k_rown)
        elif j == 2:
            for core in (0, 1):
                arrived(ret.at[2, core, 0:half], k_rfwd[1] + core)
                arrived(ret.at[2, core, half:CAP], k_rfwd[3] + core)
        else:
            for core in (0, 1):
                arrived(ret.at[j, core], k_ret[RING - j] + core)
        got = jnp.dot(gm[j], ret[j].reshape(ROWS, width), preferred_element_type=F32)
        if first:
            acc[...] = got
        else:
            acc[...] += got

    G(0)
    dispatch_forward()
    R(0)
    combine_table()
    H(0)
    G(1)
    G(3)
    F(0)
    R(1)
    R(3)
    O(0, True)
    H(1)
    H(3)
    G(2)
    F(1)
    F(3)
    R(2)
    O(1)
    O(3)
    C(0, True)
    H(2)
    F(2)
    O(2)
    C(1)
    C(3)
    return_forward()
    C(2)

    za, zb = lax.rem(z, RING), lax.div(z, RING)
    cols = width // 2
    block = tokens // RING
    sub = block // RING
    for h in range(2):
        zs[h] = acc[:, h * cols:(h + 1) * cols].astype(BF).reshape(RING, block, cols)
    zl, zr = dev_z(-1), dev_z(1)
    k = rs_start(zs, za, zl, zr, zrl, zfin)
    rs_relay(k, zs, za, zl, zr, zrl, zfin, zcmb)
    for h, v in enumerate(rs_finish(k, zs, za, zfin)):
        ys[h] = v.astype(BF).reshape(RING, sub, cols)
    yl, yr = dev_z(-4), dev_z(4)
    k = rs_start(ys, zb, yl, yr, yrl, yfin)
    rs_relay(k, ys, zb, yl, yr, yrl, yfin, ycmb)
    for h, v in enumerate(rs_finish(k, ys, zb, yfin)):
        zo[h, za, zb] = v.astype(BF)

    def far(h, i):
        return zo.at[h, za, i]

    def near(h, i):
        return zo.at[h, i]

    k = ag_start(far, zb, yl, yr)
    ag_relay(k, far, zb, yl, yr)
    ag_finish(k, far, zb)
    k = ag_start(near, za, zl, zr)
    ag_relay(k, near, za, zl, zr)
    ag_finish(k, near, za)
    for h in range(2):
        out[:, h * cols:(h + 1) * cols] = zo[h].reshape(tokens, cols)
    for copy in pending:
        copy.wait_send()


def local(tokens, route_ids, gates, w_gate, w_up, w_down):
    w_gate, w_up, w_down = w_gate[0], w_up[0], w_down[0]
    n, width = tokens.shape
    units = w_gate.shape[1]
    cols, block = width // 2, n // RING
    sub = block // RING
    V = pltpu.VMEM
    scratch = [
        V(w_gate.shape, BF), V(w_up.shape, BF), V(w_down.shape, BF),
        V((128, n), F32),
        V((RING, 2, CAP, width), BF),
        V((RING, 2, CAP, width), BF),
        V((2, 2, CAP // 2, width), BF),
        V((RING, 2, RING, PART, units), BF),
        V((RING, 2, PART, units), BF),
        V((RING, 4, PART, units), BF),
        V((RING, 2, PART, units), BF),
        V((RING, 2, RING, PART, units // 2), BF),
        V((RING, 2, CAP, width), BF),
        V((2, 2, CAP // 2, width), BF),
        V((RING, 2, CAP, width), BF),
        V((RING, n, ROWS), BF),
        V((n, width), F32),
        V((2, RING, block, cols), BF),
        V((2, block, cols), BF),
        V((4, block, cols), BF),
        V((2, block, cols), BF),
        V((2, RING, sub, cols), BF),
        V((2, sub, cols), BF),
        V((4, sub, cols), BF),
        V((2, sub, cols), BF),
        V((2, RING, RING, sub, cols), BF),
        pltpu.SemaphoreType.DMA((3,)),
        pltpu.SemaphoreType.DMA((NSEM,)),
        pltpu.SemaphoreType.DMA((NSEM,)),
        pltpu.SemaphoreType.REGULAR,
    ]
    vmem = pl.BlockSpec(memory_space=pltpu.VMEM)
    anyspace = pl.BlockSpec(memory_space=pl.ANY)
    return pl.pallas_call(
        kernel,
        out_shape=jax.ShapeDtypeStruct((n, width), BF),
        in_specs=[vmem, vmem, vmem, anyspace, anyspace, anyspace],
        out_specs=vmem,
        scratch_shapes=scratch,
        compiler_params=pltpu.CompilerParams(
            collective_id=0, has_side_effects=True, vmem_limit_bytes=48 * 1024 * 1024),
        name="expert_layer",
    )(tokens, route_ids, gates, w_gate, w_up, w_down)


def solution(mesh):
    return jax.shard_map(
        local,
        mesh=mesh,
        in_specs=(
            P("expert", "dp"),
            P("expert", None),
            P("expert", None),
            P("expert", "dp", "tensor"),
            P("expert", "dp", "tensor"),
            P("expert", "tensor", "dp"),
        ),
        out_specs=P("expert", "dp"),
        check_vma=False,
    )
```

```python
import jax
import jax.numpy as jnp
from jax import lax
from jax.experimental import pallas as pl
from jax.experimental.pallas import tpu as pltpu
from jax.sharding import PartitionSpec as P

BF = jnp.bfloat16
F32 = jnp.float32
RING = 4
CAP = 96
ROWS = 2 * CAP
PART = ROWS // RING
NONE = -1000.0
NSEM = 190
QUARTER = CAP // RING


def kernel(tok_h, route, gates, wg_h, wu_h, wd_h, out, *s):
    (tok, wg, wu, wd, slots, table, pick, rows, farpick, far_rows, part, rl, fin, cmb, hid, obuf, far_out, rhop, ret,
     far_ret, gm, acc, *zbufs) = s[:-4]
    wsem, ssem, rsem, ready = s[-4:]
    tokens, width = tok.shape
    x = lax.axis_index("dp")
    e = lax.axis_index("expert")
    z = lax.axis_index("tensor")
    y, c = lax.div(e, 2), lax.rem(e, 2)
    nz = RING * RING

    def chip(j):
        return lax.rem(y + j, RING)

    def dev_e(j, core):
        return {"expert": chip(j) * 2 + core}

    def dev_x(j):
        return {"dp": lax.rem(x + j, RING)}

    def dev_z(j):
        return {"tensor": lax.rem(z + nz + j, nz)}

    loads = [pltpu.make_async_copy(a, b, wsem.at[i])
             for i, (a, b) in enumerate(((tok_h, tok), (wg_h, wg), (wu_h, wu), (wd_h, wd)))]
    for load in loads:
        load.start()

    barrier = pltpu.get_barrier_semaphore()
    peers = [dev_e(0, 1 - c)] + [dev_e(j, k) for j in (1, 2, 3) for k in (0, 1)]
    peers += [dev_x(1), dev_x(3)] + [dev_z(j) for j in (1, -1, 2, -2, 4, -4)]
    for peer in peers:
        pl.semaphore_signal(barrier, inc=1, device_id=peer, device_id_type=pl.DeviceIdType.MESH)

    used = [0]
    pending = []

    def take(n=1):
        used[0] += n
        assert used[0] <= NSEM
        return used[0] - n

    def send(src, dst, dev, k, k_recv):
        copy = pltpu.make_async_remote_copy(
            src_ref=src, dst_ref=dst, send_sem=ssem.at[k], recv_sem=rsem.at[k_recv],
            device_id=dev, device_id_type=pl.DeviceIdType.MESH)
        copy.start()
        pending.append(copy)
        return copy

    def arrived(dst, k):
        pltpu.make_async_remote_copy(
            src_ref=dst, dst_ref=dst, send_sem=ssem.at[0], recv_sem=rsem.at[k],
            device_id=dev_e(0, 1 - c), device_id_type=pl.DeviceIdType.MESH).wait_recv()

    r0, r1 = route[0:1, :], route[1:2, :]
    line = lax.broadcasted_iota(jnp.int32, (16, tokens), 0)
    hit0, hit1 = line == r0, line == r1
    hits = jnp.where(hit0 | hit1, 1.0, 0.0)
    later = jnp.where(
        lax.broadcasted_iota(jnp.int32, (tokens, tokens), 1)
        > lax.broadcasted_iota(jnp.int32, (tokens, tokens), 0), 1.0, 0.0)
    rank = jnp.dot(hits.astype(BF), later.astype(BF), preferred_element_type=F32)
    slots[...] = jnp.where(hit0 | hit1, rank, NONE)
    table[...] = jnp.zeros_like(table)
    for n, (hit, r) in enumerate(((hit0, r0), (hit1, r1))):
        place = jnp.sum(jnp.where(hit, rank, 0.0), axis=0, keepdims=True) + r.astype(F32) * float(CAP)
        table[n:n + 1, :] = place
        table[n + 2:n + 3, :] = gates[n:n + 1, :]

    def picked(j):
        line = lax.broadcasted_iota(jnp.int32, (ROWS, tokens), 0).astype(F32)
        first = slots[pl.ds(chip(j) * 2, 1), :]
        second = slots[pl.ds(chip(j) * 2 + 1, 1), :] + float(CAP)
        chosen = jnp.where((line == first) | (line == second), 1.0, 0.0).astype(BF)
        got = jnp.dot(chosen, tok[...], preferred_element_type=F32).astype(BF)
        pick[j] = got.reshape(2, CAP, width)

    ks_d = {j: take(2) for j in (1, 3)}
    k_far = take(2)
    k_spread = take(4)
    k_own = take()
    za, zb = lax.rem(z, RING), lax.div(z, RING)

    loads[0].wait()
    line = lax.broadcasted_iota(jnp.int32, (2 * QUARTER, tokens), 0)
    slot = jnp.where(line < QUARTER, line, line - QUARTER) + za * QUARTER
    place = jnp.where(line < QUARTER, slots[pl.ds(chip(2) * 2, 1), :], slots[pl.ds(chip(2) * 2 + 1, 1), :])
    chosen = jnp.where(slot.astype(F32) == place, 1.0, 0.0).astype(BF)
    got = jnp.dot(chosen, tok[...], preferred_element_type=F32).astype(BF)
    farpick[...] = got.reshape(2, QUARTER, width)
    pl.semaphore_wait(barrier, len(peers))
    for core in (0, 1):
        send(farpick.at[core], far_rows.at[za, c], dev_e(2, core), k_far + core, k_far + c)
    for j in (4, -4):
        pl.semaphore_signal(ready, inc=1, device_id=dev_z(j), device_id_type=pl.DeviceIdType.MESH)
    for j in (3, 1):
        picked(j)
        for core in (0, 1):
            send(pick.at[j, core], rows.at[RING - j, c], dev_e(j, core), ks_d[j] + core, ks_d[j] + c)
    picked(0)
    send(pick.at[0, 1 - c], rows.at[0, c], dev_e(0, 1 - c), k_own, k_own)
    rows[0, c] = pick[0, c]

    def far_spread():
        for core in (0, 1):
            arrived(far_rows.at[za, core], k_far + core)
        for n, j in enumerate((1, -1)):
            send(far_rows.at[za], far_rows.at[za], dev_z(j), k_spread + n, k_spread + n)
        for n, j in enumerate((2, -2)):
            send(far_rows.at[za, n], far_rows.at[za, n], dev_z(j), k_spread + 2 + n, k_spread + 2 + n)

    def rows_here(j):
        if j == 0:
            arrived(rows.at[0, 1 - c], k_own)
        elif j == 2:
            arrived(far_rows.at[lax.rem(za + 3, RING)], k_spread)
            arrived(far_rows.at[lax.rem(za + 1, RING)], k_spread + 1)
            for n in (0, 1):
                arrived(far_rows.at[lax.rem(za + 2, RING), n], k_spread + 2 + n)
        else:
            for core in (0, 1):
                arrived(rows.at[j, core], ks_d[RING - j] + core)

    def rs_start(own, i, left, right, bufs):
        k = take(6)
        relay, done, _ = bufs
        opp, r, l = lax.rem(i + 2, RING), lax.rem(i + 1, RING), lax.rem(i + 3, RING)
        send(own[0].at[opp], relay[0], right, k, k)
        send(own[1].at[opp], relay[1], left, k + 1, k + 1)
        send(own[1].at[r], done[0], right, k + 2, k + 2)
        send(own[0].at[l], done[1], left, k + 3, k + 3)
        return k

    def rs_relay(k, own, i, left, right, bufs):
        relay, done, mixed = bufs
        r, l = lax.rem(i + 1, RING), lax.rem(i + 3, RING)
        arrived(relay[0], k)
        mixed[0][...] = (own[0][r].astype(F32) + relay[0][...].astype(F32)).astype(BF)
        send(mixed[0], done[2], right, k + 4, k + 4)
        arrived(relay[1], k + 1)
        mixed[1][...] = (own[1][l].astype(F32) + relay[1][...].astype(F32)).astype(BF)
        send(mixed[1], done[3], left, k + 5, k + 5)

    def rs_finish(k, own, i, bufs):
        done = bufs[1]
        for n in range(4):
            arrived(done[n], k + 2 + n)
        first = own[0][i].astype(F32) + done[1][...].astype(F32) + done[2][...].astype(F32)
        second = own[1][i].astype(F32) + done[0][...].astype(F32) + done[3][...].astype(F32)
        return first, second

    def ag_start(at, i, left, right):
        k = take(6)
        send(at(0, i), at(0, i), right, k, k)
        send(at(1, i), at(1, i), left, k + 1, k + 1)
        send(at(1, i), at(1, i), right, k + 2, k + 2)
        send(at(0, i), at(0, i), left, k + 3, k + 3)
        return k

    def ag_relay(k, at, i, left, right):
        r, l = lax.rem(i + 1, RING), lax.rem(i + 3, RING)
        arrived(at(0, l), k)
        send(at(0, l), at(0, l), right, k + 4, k + 4)
        arrived(at(1, r), k + 1)
        send(at(1, r), at(1, r), left, k + 5, k + 5)

    def ag_finish(k, at, i):
        opp, r, l = lax.rem(i + 2, RING), lax.rem(i + 1, RING), lax.rem(i + 3, RING)
        arrived(at(1, l), k + 2)
        arrived(at(0, r), k + 3)
        arrived(at(0, opp), k + 4)
        arrived(at(1, opp), k + 5)

    xl, xr = dev_x(3), dev_x(1)
    rs_k, ag_k = {}, {}

    def xbufs(j):
        return ([rl.at[j, h] for h in range(2)], [fin.at[j, n] for n in range(4)],
                [cmb.at[j, h] for h in range(2)])

    def xown(j):
        return [part.at[j, h] for h in range(2)]

    def hid_at(j):
        return lambda h, i: hid.at[j, h, i]

    def G(j):
        rows_here(j)
        if j == 0:
            loads[1].wait()
            loads[2].wait()
        here = (far_rows if j == 2 else rows.at[j])[...].reshape(ROWS, width)
        for n, w in enumerate((wg, wu)):
            got = jnp.dot(here, w[...], preferred_element_type=F32).astype(BF)
            part[j, n] = got.reshape(RING, PART, got.shape[1])
        rs_k[j] = rs_start(xown(j), x, xl, xr, xbufs(j))

    def R(j):
        rs_relay(rs_k[j], xown(j), x, xl, xr, xbufs(j))

    def H(j):
        gate, up = rs_finish(rs_k[j], xown(j), x, xbufs(j))
        got = (gate / (1.0 + jnp.exp(-gate)) * up).astype(BF)
        hw = got.shape[1] // 2
        hid[j, 0, x] = got[:, :hw]
        hid[j, 1, x] = got[:, hw:]
        ag_k[j] = ag_start(hid_at(j), x, xl, xr)

    def F(j):
        ag_relay(ag_k[j], hid_at(j), x, xl, xr)

    k_ret = {j: take(2) for j in (1, 3)}
    k_rhop = take(4)
    k_rfwd = {1: take(4), 3: take(4)}
    k_rown = take()

    def O(j, first_use=False):
        ag_finish(ag_k[j], hid_at(j), x)
        if first_use:
            loads[3].wait()
        hw = wd.shape[0] // 2
        got = jnp.dot(hid[j, 0].reshape(ROWS, hw), wd[0:hw], preferred_element_type=F32)
        got += jnp.dot(hid[j, 1].reshape(ROWS, hw), wd[hw:], preferred_element_type=F32)
        got = got.astype(BF)
        if j == 2:
            far_out[...] = got.reshape(far_out.shape)
            for a in (0, 1):
                for n in (0, 1):
                    send(far_out.at[2 * n + a], rhop.at[n, a], dev_e(1 + 2 * n, c), k_rhop + 2 * n + a, k_rhop + 2 * n + a)
            return
        obuf[j] = got.reshape(2, CAP, width)
        if j == 0:
            send(obuf.at[0, 1 - c], ret.at[0, c], dev_e(0, 1 - c), k_rown, k_rown)
            ret[0, c] = obuf[0, c]
        else:
            for core in (0, 1):
                send(obuf.at[j, core], ret.at[RING - j, c], dev_e(j, core), k_ret[j] + core, k_ret[j] + c)

    def return_forward():
        for a in (0, 1):
            for n in (0, 1):
                arrived(rhop.at[n, a], k_rhop + 2 * n + a)
                k = k_rfwd[1 + 2 * n] + 2 * a
                for core in (0, 1):
                    send(rhop.at[n, a, core], far_ret.at[c, 2 * n + a], dev_e(1 + 2 * n, core), k + core, k + c)

    def combine_table():
        by_token = table[...].T
        column = lax.broadcasted_iota(jnp.int32, (tokens, ROWS), 1)
        for j in range(RING):
            here = (column + chip(j) * ROWS).astype(F32)
            weight = jnp.where(here == by_token[:, 0:1], by_token[:, 2:3], 0.0)
            weight += jnp.where(here == by_token[:, 1:2], by_token[:, 3:4], 0.0)
            gm[j] = weight.astype(BF)

    def C(j, first=False):
        if j == 0:
            arrived(ret.at[0, 1 - c], k_rown)
        elif j == 2:
            for a in (0, 1):
                for n in (0, 1):
                    for core in (0, 1):
                        arrived(far_ret.at[core, 2 * n + a], k_rfwd[1 + 2 * n] + 2 * a + core)
        else:
            for core in (0, 1):
                arrived(ret.at[j, core], k_ret[RING - j] + core)
        back = (far_ret if j == 2 else ret.at[j])[...].reshape(ROWS, width)
        got = jnp.dot(gm[j], back, preferred_element_type=F32)
        if first:
            acc[...] = got
        else:
            acc[...] += got

    G(0)
    combine_table()
    R(0)
    far_spread()
    H(0)
    G(1)
    G(3)
    F(0)
    R(1)
    R(3)
    G(2)
    O(0, True)
    H(1)
    R(2)
    H(3)
    F(1)
    F(3)
    H(2)
    O(1)
    O(3)
    C(0, True)
    F(2)
    O(2)
    C(1)
    C(3)
    return_forward()
    C(2)

    block = tokens // RING
    sub = block // RING
    cols = width // 2
    near_r, near_l, near_rr, near_ll = dev_z(1), dev_z(-1), dev_z(2), dev_z(-2)
    far_devs = (dev_z(4), dev_z(-4), dev_z(8))
    streams = [zbufs[6 * q:6 * q + 6] for q in range(2)]
    ks_near, ks_sum, ks_far, ks_out = [[take(n) for _ in range(2)] for n in (4, 3, 3, 3 * RING)]

    def ring(i, j):
        return lax.rem(i + RING + j, RING)

    for q, (mine, one, two, mid, far_in, done) in enumerate(streams):
        mine[...] = acc[:, q * cols:(q + 1) * cols].astype(BF).reshape(mine.shape)
        k = ks_near[q]
        send(mine.at[ring(za, 2), 0], two.at[0], near_rr, k + 2, k + 2)
        send(mine.at[ring(za, 2), 1], two.at[1], near_ll, k + 3, k + 3)
        send(mine.at[ring(za, 1)], one.at[0], near_r, k, k)
        send(mine.at[ring(za, -1)], one.at[1], near_l, k + 1, k + 1)
    pl.semaphore_wait(ready, 2)
    for q, (mine, one, two, mid, far_in, done) in enumerate(streams):
        k = ks_near[q]
        for n in (0, 1):
            arrived(two.at[n], k + 2 + n)
            arrived(one.at[n], k + n)
        total = mine[za].astype(F32) + one[0].astype(F32) + one[1].astype(F32) + two[...].astype(F32)
        mid[...] = total.astype(BF).reshape(mid.shape)
        for n in (2, 0, 1):
            send(mid.at[ring(zb, (1, -1, 2)[n])], far_in.at[n], far_devs[n], ks_sum[q] + n, ks_sum[q] + n)

    def spread(q, b):
        done = streams[q][5]
        k = ks_out[q] + 3 * b
        ref = done.at[za, b]
        send(ref, ref, near_r, k, k)
        send(ref, ref, near_l, k + 1, k + 1)
        send(ref, ref, dev_z(2 - 4 * lax.div(b, 2)), k + 2, k + 2)

    for q, (mine, one, two, mid, far_in, done) in enumerate(streams):
        for n in (0, 1, 2):
            arrived(far_in.at[n], ks_sum[q] + n)
        total = mid[zb].astype(F32) + far_in[0].astype(F32) + far_in[1].astype(F32) + far_in[2].astype(F32)
        done[za, zb] = total.astype(BF)
        for n in (2, 0, 1):
            send(done.at[za, zb], done.at[za, zb], far_devs[n], ks_far[q] + n, ks_far[q] + n)
        spread(q, zb)
    for n in (0, 1, 2):
        for q in range(2):
            b = ring(zb, (-1, 1, 2)[n])
            arrived(streams[q][5].at[za, b], ks_far[q] + n)
            spread(q, b)
    for q in range(2):
        done = streams[q][5]
        for b in range(RING):
            for n, j in enumerate((-1, 1, 2)):
                arrived(done.at[ring(za, j), b], ks_out[q] + 3 * b + n)
        out[:, q * cols:(q + 1) * cols] = done[...].reshape(tokens, cols)
    for copy in pending:
        copy.wait_send()


def local(tokens, route_ids, gates, w_gate, w_up, w_down):
    w_gate, w_up, w_down = w_gate[0], w_up[0], w_down[0]
    n, width = tokens.shape
    units = w_gate.shape[1]
    block = n // RING
    sub = block // RING
    V = pltpu.VMEM
    zbufs = []
    for _ in range(2):
        cols = width // 2
        zbufs += [V((RING, 2, block // 2, cols), BF), V((2, 2, block // 2, cols), BF),
                  V((2, block // 2, cols), BF), V((RING, sub, cols), BF),
                  V((3, sub, cols), BF), V((RING, RING, sub, cols), BF)]
    scratch = [
        V(tokens.shape, BF), V(w_gate.shape, BF), V(w_up.shape, BF), V(w_down.shape, BF),
        V((16, n), F32),
        V((128, n), F32),
        V((RING, 2, CAP, width), BF),
        V((RING, 2, CAP, width), BF),
        V((2, QUARTER, width), BF),
        V((RING, 2, QUARTER, width), BF),
        V((RING, 2, RING, PART, units), BF),
        V((RING, 2, PART, units), BF),
        V((RING, 4, PART, units), BF),
        V((RING, 2, PART, units), BF),
        V((RING, 2, RING, PART, units // 2), BF),
        V((RING, 2, CAP, width), BF),
        V((RING, 2, QUARTER, width), BF),
        V((2, 2, 2, QUARTER, width), BF),
        V((RING, 2, CAP, width), BF),
        V((2, RING, QUARTER, width), BF),
        V((RING, n, ROWS), BF),
        V((n, width), F32),
        *zbufs,
        pltpu.SemaphoreType.DMA((4,)),
        pltpu.SemaphoreType.DMA((NSEM,)),
        pltpu.SemaphoreType.DMA((NSEM,)),
        pltpu.SemaphoreType.REGULAR,
    ]
    vmem = pl.BlockSpec(memory_space=pltpu.VMEM)
    hbm = pl.BlockSpec(memory_space=pltpu.HBM)
    return pl.pallas_call(
        kernel,
        out_shape=jax.ShapeDtypeStruct((n, width), BF),
        in_specs=[hbm, vmem, vmem, hbm, hbm, hbm],
        out_specs=vmem,
        scratch_shapes=scratch,
        compiler_params=pltpu.CompilerParams(
            collective_id=0, has_side_effects=True, vmem_limit_bytes=66400000),
        name="expert_layer",
    )(tokens, route_ids.T, gates.T, w_gate, w_up, w_down)


def solution(mesh):
    return jax.shard_map(
        local,
        mesh=mesh,
        in_specs=(
            P("expert", "dp"),
            P("expert", None),
            P("expert", None),
            P("expert", "dp", "tensor"),
            P("expert", "dp", "tensor"),
            P("expert", "tensor", "dp"),
        ),
        out_specs=P("expert", "dp"),
        check_vma=False,
    )
```

```python
import jax
import jax.numpy as jnp
from jax import lax
from jax.experimental import pallas as pl
from jax.experimental.pallas import tpu as pltpu
from jax.sharding import PartitionSpec as P

BF = jnp.bfloat16
F32 = jnp.float32
RING = 4
CAP = 96
ROWS = 2 * CAP
PART = ROWS // RING
NONE = -1000.0
NSEM = 190
QUARTER = CAP // RING


def kernel(tok_h, route_h, gates_h, wg_h, wu_h, wd_h, out, *s):
    (route, gates, tok, wg, wu, wd, slots, table, pick, rows, farpick, far_rows, part, rl, fin, cmb, hid, obuf, far_out, rhop, ret,
     far_ret, gm, acc, *zbufs) = s[:-4]
    wsem, ssem, rsem, ready = s[-4:]
    tokens, width = tok.shape
    x = lax.axis_index("dp")
    e = lax.axis_index("expert")
    z = lax.axis_index("tensor")
    y, c = lax.div(e, 2), lax.rem(e, 2)
    nz = RING * RING

    def chip(j):
        return lax.rem(y + j, RING)

    def dev_e(j, core):
        return {"expert": chip(j) * 2 + core}

    def dev_x(j):
        return {"dp": lax.rem(x + j, RING)}

    def dev_z(j):
        return {"tensor": lax.rem(z + nz + j, nz)}

    loads = [pltpu.make_async_copy(a, b, wsem.at[i])
             for i, (a, b) in enumerate(((route_h, route), (gates_h, gates), (tok_h, tok), (wg_h, wg),
                                    (wu_h, wu), (wd_h, wd)))]
    for load in loads:
        load.start()

    barrier = pltpu.get_barrier_semaphore()
    peers = [dev_e(0, 1 - c)] + [dev_e(j, k) for j in (1, 2, 3) for k in (0, 1)]
    peers += [dev_x(1), dev_x(3)] + [dev_z(j) for j in (1, -1, 2, -2)]
    for peer in peers:
        pl.semaphore_signal(barrier, inc=1, device_id=peer, device_id_type=pl.DeviceIdType.MESH)

    used = [0]
    pending = []

    def take(n=1):
        used[0] += n
        assert used[0] <= NSEM
        return used[0] - n

    def send(src, dst, dev, k, k_recv):
        copy = pltpu.make_async_remote_copy(
            src_ref=src, dst_ref=dst, send_sem=ssem.at[k], recv_sem=rsem.at[k_recv],
            device_id=dev, device_id_type=pl.DeviceIdType.MESH)
        copy.start()
        pending.append(copy)
        return copy

    def arrived(dst, k):
        pltpu.make_async_remote_copy(
            src_ref=dst, dst_ref=dst, send_sem=ssem.at[0], recv_sem=rsem.at[k],
            device_id=dev_e(0, 1 - c), device_id_type=pl.DeviceIdType.MESH).wait_recv()

    loads[0].wait()
    loads[1].wait()
    r0, r1 = route[0:1, :], route[1:2, :]
    line = lax.broadcasted_iota(jnp.int32, (16, tokens), 0)
    hit0, hit1 = line == r0, line == r1
    hits = jnp.where(hit0 | hit1, 1.0, 0.0)
    later = jnp.where(
        lax.broadcasted_iota(jnp.int32, (tokens, tokens), 1)
        > lax.broadcasted_iota(jnp.int32, (tokens, tokens), 0), 1.0, 0.0)
    rank = jnp.dot(hits.astype(BF), later.astype(BF), preferred_element_type=F32)
    slots[...] = jnp.where(hit0 | hit1, rank, NONE)
    table[...] = jnp.zeros_like(table)
    for n, (hit, r) in enumerate(((hit0, r0), (hit1, r1))):
        place = jnp.sum(jnp.where(hit, rank, 0.0), axis=0, keepdims=True) + r.astype(F32) * float(CAP)
        table[n:n + 1, :] = place
        table[n + 2:n + 3, :] = gates[n:n + 1, :]

    def picked(j):
        line = lax.broadcasted_iota(jnp.int32, (ROWS, tokens), 0).astype(F32)
        first = slots[pl.ds(chip(j) * 2, 1), :]
        second = slots[pl.ds(chip(j) * 2 + 1, 1), :] + float(CAP)
        chosen = jnp.where((line == first) | (line == second), 1.0, 0.0).astype(BF)
        got = jnp.dot(chosen, tok[...], preferred_element_type=F32).astype(BF)
        pick[j] = got.reshape(2, CAP, width)

    ks_d = {j: take(2) for j in (1, 3)}
    k_far = take(2)
    k_spread = take(4)
    k_own = take()
    za, zb = lax.rem(z, RING), lax.div(z, RING)

    loads[2].wait()
    line = lax.broadcasted_iota(jnp.int32, (2 * QUARTER, tokens), 0)
    slot = jnp.where(line < QUARTER, line, line - QUARTER) + za * QUARTER
    place = jnp.where(line < QUARTER, slots[pl.ds(chip(2) * 2, 1), :], slots[pl.ds(chip(2) * 2 + 1, 1), :])
    chosen = jnp.where(slot.astype(F32) == place, 1.0, 0.0).astype(BF)
    got = jnp.dot(chosen, tok[...], preferred_element_type=F32).astype(BF)
    farpick[...] = got.reshape(2, QUARTER, width)
    for j in (3, 1, 0):
        picked(j)
    pl.semaphore_wait(barrier, len(peers))
    for core in (0, 1):
        send(farpick.at[core], far_rows.at[za, c], dev_e(2, core), k_far + core, k_far + c)
    for j in (3, 1):
        for core in (0, 1):
            send(pick.at[j, core], rows.at[RING - j, c], dev_e(j, core), ks_d[j] + core, ks_d[j] + c)
    send(pick.at[0, 1 - c], rows.at[0, c], dev_e(0, 1 - c), k_own, k_own)
    rows[0, c] = pick[0, c]

    def vouch(n, hops):
        for j in (hops, -hops):
            pl.semaphore_signal(ready.at[n], inc=1, device_id=dev_z(j), device_id_type=pl.DeviceIdType.MESH)

    vouch(0, 2)

    def far_spread():
        for core in (0, 1):
            arrived(far_rows.at[za, core], k_far + core)
        for n, j in enumerate((1, -1)):
            send(far_rows.at[za], far_rows.at[za], dev_z(j), k_spread + n, k_spread + n)
        for n, j in enumerate((2, -2)):
            send(far_rows.at[za, n], far_rows.at[za, n], dev_z(j), k_spread + 2 + n, k_spread + 2 + n)

    def rows_here(j):
        if j == 0:
            arrived(rows.at[0, 1 - c], k_own)
        elif j == 2:
            arrived(far_rows.at[lax.rem(za + 3, RING)], k_spread)
            arrived(far_rows.at[lax.rem(za + 1, RING)], k_spread + 1)
            for n in (0, 1):
                arrived(far_rows.at[lax.rem(za + 2, RING), n], k_spread + 2 + n)
        else:
            for core in (0, 1):
                arrived(rows.at[j, core], ks_d[RING - j] + core)

    def rs_start(own, i, left, right, bufs):
        k = take(6)
        relay, done, _ = bufs
        opp, r, l = lax.rem(i + 2, RING), lax.rem(i + 1, RING), lax.rem(i + 3, RING)
        send(own[0].at[opp], relay[0], right, k, k)
        send(own[1].at[opp], relay[1], left, k + 1, k + 1)
        send(own[1].at[r], done[0], right, k + 2, k + 2)
        send(own[0].at[l], done[1], left, k + 3, k + 3)
        return k

    def rs_relay(k, own, i, left, right, bufs):
        relay, done, mixed = bufs
        r, l = lax.rem(i + 1, RING), lax.rem(i + 3, RING)
        arrived(relay[0], k)
        mixed[0][...] = (own[0][r].astype(F32) + relay[0][...].astype(F32)).astype(BF)
        send(mixed[0], done[2], right, k + 4, k + 4)
        arrived(relay[1], k + 1)
        mixed[1][...] = (own[1][l].astype(F32) + relay[1][...].astype(F32)).astype(BF)
        send(mixed[1], done[3], left, k + 5, k + 5)

    def rs_finish(k, own, i, bufs):
        done = bufs[1]
        for n in range(4):
            arrived(done[n], k + 2 + n)
        first = own[0][i].astype(F32) + done[1][...].astype(F32) + done[2][...].astype(F32)
        second = own[1][i].astype(F32) + done[0][...].astype(F32) + done[3][...].astype(F32)
        return first, second

    def ag_start(at, i, left, right):
        k = take(6)
        send(at(0, i), at(0, i), right, k, k)
        send(at(1, i), at(1, i), left, k + 1, k + 1)
        send(at(1, i), at(1, i), right, k + 2, k + 2)
        send(at(0, i), at(0, i), left, k + 3, k + 3)
        return k

    def ag_relay(k, at, i, left, right):
        r, l = lax.rem(i + 1, RING), lax.rem(i + 3, RING)
        arrived(at(0, l), k)
        send(at(0, l), at(0, l), right, k + 4, k + 4)
        arrived(at(1, r), k + 1)
        send(at(1, r), at(1, r), left, k + 5, k + 5)

    def ag_finish(k, at, i):
        opp, r, l = lax.rem(i + 2, RING), lax.rem(i + 1, RING), lax.rem(i + 3, RING)
        arrived(at(1, l), k + 2)
        arrived(at(0, r), k + 3)
        arrived(at(0, opp), k + 4)
        arrived(at(1, opp), k + 5)

    xl, xr = dev_x(3), dev_x(1)
    rs_k, ag_k = {}, {}

    def xbufs(j):
        return ([rl.at[j, h] for h in range(2)], [fin.at[j, n] for n in range(4)],
                [cmb.at[j, h] for h in range(2)])

    def xown(j):
        return [part.at[j, h] for h in range(2)]

    def hid_at(j):
        return lambda h, i: hid.at[j, h, i]

    def G(j):
        rows_here(j)
        if j == 0:
            loads[3].wait()
            loads[4].wait()
        here = (far_rows if j == 2 else rows.at[j])[...].reshape(ROWS, width)
        for n, w in enumerate((wg, wu)):
            got = jnp.dot(here, w[...], preferred_element_type=F32).astype(BF)
            part[j, n] = got.reshape(RING, PART, got.shape[1])
        rs_k[j] = rs_start(xown(j), x, xl, xr, xbufs(j))

    def R(j):
        rs_relay(rs_k[j], xown(j), x, xl, xr, xbufs(j))

    def H(j):
        gate, up = rs_finish(rs_k[j], xown(j), x, xbufs(j))
        got = (gate / (1.0 + jnp.exp(-gate)) * up).astype(BF)
        hw = got.shape[1] // 2
        hid[j, 0, x] = got[:, :hw]
        hid[j, 1, x] = got[:, hw:]
        ag_k[j] = ag_start(hid_at(j), x, xl, xr)

    def F(j):
        ag_relay(ag_k[j], hid_at(j), x, xl, xr)

    k_ret = {j: take(2) for j in (1, 3)}
    k_rhop = take(4)
    k_rfwd = take(8)
    cols = width // 2
    k_rown = take()

    def O(j, first_use=False):
        ag_finish(ag_k[j], hid_at(j), x)
        if first_use:
            loads[5].wait()
        hw = wd.shape[0] // 2
        got = jnp.dot(hid[j, 0].reshape(ROWS, hw), wd[0:hw], preferred_element_type=F32)
        got += jnp.dot(hid[j, 1].reshape(ROWS, hw), wd[hw:], preferred_element_type=F32)
        got = got.astype(BF)
        if j == 2:
            for q in (0, 1):
                far_out[q] = got[:, q * cols:(q + 1) * cols].reshape(far_out.shape[1:])
                for n in (0, 1):
                    k = k_rhop + 2 * q + n
                    send(far_out.at[q, 2 * n:2 * n + 2], rhop.at[q, n], dev_e(1 + 2 * n, c), k, k)
            return
        obuf[j] = got.reshape(2, CAP, width)
        if j == 0:
            send(obuf.at[0, 1 - c], ret.at[0, c], dev_e(0, 1 - c), k_rown, k_rown)
            ret[0, c] = obuf[0, c]
        else:
            for core in (0, 1):
                send(obuf.at[j, core], ret.at[RING - j, c], dev_e(j, core), k_ret[j] + core, k_ret[j] + c)

    def return_forward(q):
        for n in (0, 1):
            arrived(rhop.at[q, n], k_rhop + 2 * q + n)
            k = k_rfwd + 4 * q + 2 * n
            for core in (0, 1):
                send(rhop.at[q, n, :, core], far_ret.at[q, c, 2 * n:2 * n + 2], dev_e(1 + 2 * n, core), k + core, k + c)

    def combine_table():
        by_token = table[...].T
        column = lax.broadcasted_iota(jnp.int32, (tokens, ROWS), 1)
        for j in range(RING):
            here = (column + chip(j) * ROWS).astype(F32)
            weight = jnp.where(here == by_token[:, 0:1], by_token[:, 2:3], 0.0)
            weight += jnp.where(here == by_token[:, 1:2], by_token[:, 3:4], 0.0)
            gm[j] = weight.astype(BF)

    def C(j, first=False):
        if j == 0:
            arrived(ret.at[0, 1 - c], k_rown)
        else:
            for core in (0, 1):
                arrived(ret.at[j, core], k_ret[RING - j] + core)
        got = jnp.dot(gm[j], ret[j].reshape(ROWS, width), preferred_element_type=F32)
        if first:
            acc[...] = got
        else:
            acc[...] += got

    G(0)
    combine_table()
    pl.semaphore_wait(ready.at[0], 2)
    vouch(1, 4)
    R(0)
    far_spread()
    H(0)
    G(1)
    G(3)
    F(0)
    R(1)
    R(3)
    G(2)
    O(0, True)
    H(1)
    R(2)
    H(3)
    F(1)
    F(3)
    H(2)
    O(1)
    O(3)
    C(0, True)
    F(2)
    O(2)
    C(1)
    C(3)
    return_forward(0)
    return_forward(1)

    block = tokens // RING
    sub = block // RING
    near_r, near_l, near_rr, near_ll = dev_z(1), dev_z(-1), dev_z(2), dev_z(-2)
    far_devs = (dev_z(4), dev_z(-4), dev_z(8))
    streams = [zbufs[6 * q:6 * q + 6] for q in range(2)]
    ks_near, ks_sum, ks_far, ks_out = [[take(n) for _ in range(2)] for n in (4, 3, 3, 3 * RING)]

    def ring(i, j):
        return lax.rem(i + RING + j, RING)

    for q, (mine, one, two, mid, far_in, done) in enumerate(streams):
        for n in (0, 1):
            for core in (0, 1):
                arrived(far_ret.at[q, core, 2 * n:2 * n + 2], k_rfwd + 4 * q + 2 * n + core)
        got = jnp.dot(gm[2], far_ret[q].reshape(ROWS, cols), preferred_element_type=F32)
        mine[...] = (acc[:, q * cols:(q + 1) * cols] + got).astype(BF).reshape(mine.shape)
        k = ks_near[q]
        send(mine.at[ring(za, 2), 0], two.at[0], near_rr, k + 2, k + 2)
        send(mine.at[ring(za, 2), 1], two.at[1], near_ll, k + 3, k + 3)
        send(mine.at[ring(za, 1)], one.at[0], near_r, k, k)
        send(mine.at[ring(za, -1)], one.at[1], near_l, k + 1, k + 1)
    pl.semaphore_wait(ready.at[1], 2)
    for q, (mine, one, two, mid, far_in, done) in enumerate(streams):
        k = ks_near[q]
        for n in (0, 1):
            arrived(two.at[n], k + 2 + n)
            arrived(one.at[n], k + n)
        total = mine[za].astype(F32) + one[0].astype(F32) + one[1].astype(F32) + two[...].astype(F32)
        mid[...] = total.astype(BF).reshape(mid.shape)
        for n in (2, 0, 1):
            send(mid.at[ring(zb, (1, -1, 2)[n])], far_in.at[n], far_devs[n], ks_sum[q] + n, ks_sum[q] + n)

    def spread(q, b):
        done = streams[q][5]
        k = ks_out[q] + 3 * b
        ref = done.at[za, b]
        send(ref, ref, near_r, k, k)
        send(ref, ref, near_l, k + 1, k + 1)
        send(ref, ref, dev_z(2 - 4 * lax.div(b, 2)), k + 2, k + 2)

    for q, (mine, one, two, mid, far_in, done) in enumerate(streams):
        for n in (0, 1, 2):
            arrived(far_in.at[n], ks_sum[q] + n)
        total = mid[zb].astype(F32) + far_in[0].astype(F32) + far_in[1].astype(F32) + far_in[2].astype(F32)
        done[za, zb] = total.astype(BF)
        for n in (2, 0, 1):
            send(done.at[za, zb], done.at[za, zb], far_devs[n], ks_far[q] + n, ks_far[q] + n)
        spread(q, zb)
    for n in (0, 1, 2):
        for q in range(2):
            b = ring(zb, (-1, 1, 2)[n])
            arrived(streams[q][5].at[za, b], ks_far[q] + n)
            spread(q, b)
    for q in range(2):
        done = streams[q][5]
        for b in range(RING):
            for n, j in enumerate((-1, 1, 2)):
                arrived(done.at[ring(za, j), b], ks_out[q] + 3 * b + n)
        out[:, q * cols:(q + 1) * cols] = done[...].reshape(tokens, cols)
    for copy in pending:
        copy.wait_send()


def local(tokens, route_ids, gates, w_gate, w_up, w_down):
    w_gate, w_up, w_down = w_gate[0], w_up[0], w_down[0]
    n, width = tokens.shape
    units = w_gate.shape[1]
    block = n // RING
    sub = block // RING
    V = pltpu.VMEM
    zbufs = []
    for _ in range(2):
        cols = width // 2
        zbufs += [V((RING, 2, block // 2, cols), BF), V((2, 2, block // 2, cols), BF),
                  V((2, block // 2, cols), BF), V((RING, sub, cols), BF),
                  V((3, sub, cols), BF), V((RING, RING, sub, cols), BF)]
    scratch = [
        V((2, n), jnp.int32), V((2, n), F32),
        V(tokens.shape, BF), V(w_gate.shape, BF), V(w_up.shape, BF), V(w_down.shape, BF),
        V((16, n), F32),
        V((128, n), F32),
        V((RING, 2, CAP, width), BF),
        V((RING, 2, CAP, width), BF),
        V((2, QUARTER, width), BF),
        V((RING, 2, QUARTER, width), BF),
        V((RING, 2, RING, PART, units), BF),
        V((RING, 2, PART, units), BF),
        V((RING, 4, PART, units), BF),
        V((RING, 2, PART, units), BF),
        V((RING, 2, RING, PART, units // 2), BF),
        V((RING, 2, CAP, width), BF),
        V((2, RING, 2, QUARTER, width // 2), BF),
        V((2, 2, 2, 2, QUARTER, width // 2), BF),
        V((RING, 2, CAP, width), BF),
        V((2, 2, RING, QUARTER, width // 2), BF),
        V((RING, n, ROWS), BF),
        V((n, width), F32),
        *zbufs,
        pltpu.SemaphoreType.DMA((6,)),
        pltpu.SemaphoreType.DMA((NSEM,)),
        pltpu.SemaphoreType.DMA((NSEM,)),
        pltpu.SemaphoreType.REGULAR((2,)),
    ]
    vmem = pl.BlockSpec(memory_space=pltpu.VMEM)
    hbm = pl.BlockSpec(memory_space=pltpu.HBM)
    return pl.pallas_call(
        kernel,
        out_shape=jax.ShapeDtypeStruct((n, width), BF),
        in_specs=[hbm] * 6,
        out_specs=vmem,
        scratch_shapes=scratch,
        compiler_params=pltpu.CompilerParams(
            collective_id=0, has_side_effects=True, vmem_limit_bytes=40 * 1024 * 1024),
        name="expert_layer",
    )(*[pltpu.with_memory_space_constraint(v, pltpu.HBM)
        for v in (tokens, route_ids.T, gates.T, w_gate, w_up, w_down)])


def solution(mesh):
    return jax.shard_map(
        local,
        mesh=mesh,
        in_specs=(
            P("expert", "dp"),
            P("expert", None),
            P("expert", None),
            P("expert", "dp", "tensor"),
            P("expert", "dp", "tensor"),
            P("expert", "tensor", "dp"),
        ),
        out_specs=P("expert", "dp"),
        check_vma=False,
    )
```

```python
import jax
import jax.numpy as jnp
from jax import lax
from jax.experimental import pallas as pl
from jax.experimental.pallas import tpu as pltpu
from jax.sharding import PartitionSpec as P

BF = jnp.bfloat16
F32 = jnp.float32
RING = 4
CAP = 96
ROWS = 2 * CAP
PART = ROWS // RING
NONE = -1000.0
NSEM = 190
QUARTER = CAP // RING
ROUTED_SUM = (2,)
ROUTED_GATHER = (2,)


def kernel(tok_h, route_h, gates_h, wg_h, wu_h, wd_h, out, *s):
    (route, gates, tok, wg, wu, wd, slots, table, pick, rows, farpick, far_rows, part, rl, fin, cmb, hid, obuf, far_out, ret,
     far_ret, gm, acc, *zbufs) = s[:-4]
    wsem, ssem, rsem, ready = s[-4:]
    tokens, width = tok.shape
    x = lax.axis_index("dp")
    e = lax.axis_index("expert")
    z = lax.axis_index("tensor")
    y, c = lax.div(e, 2), lax.rem(e, 2)
    nz = RING * RING

    def chip(j):
        return lax.rem(y + j, RING)

    def dev_e(j, core):
        return {"expert": chip(j) * 2 + core}

    def dev_x(j):
        return {"dp": lax.rem(x + j, RING)}

    def dev_z(j):
        return {"tensor": lax.rem(z + nz + j, nz)}

    loads = [pltpu.make_async_copy(a, b, wsem.at[i])
             for i, (a, b) in enumerate(((route_h, route), (gates_h, gates), (tok_h, tok), (wg_h, wg),
                                    (wu_h, wu), (wd_h, wd)))]
    for load in loads:
        load.start()

    barrier = pltpu.get_barrier_semaphore()
    peers = [dev_e(0, 1 - c)] + [dev_e(j, k) for j in (1, 2, 3) for k in (0, 1)]
    peers += [dev_x(1), dev_x(2), dev_x(3)] + [dev_z(j) for j in (1, -1, 2, -2)]
    for peer in peers:
        pl.semaphore_signal(barrier, inc=1, device_id=peer, device_id_type=pl.DeviceIdType.MESH)

    used = [0]
    pending = []

    def take(n=1):
        used[0] += n
        assert used[0] <= NSEM
        return used[0] - n

    def send(src, dst, dev, k, k_recv):
        copy = pltpu.make_async_remote_copy(
            src_ref=src, dst_ref=dst, send_sem=ssem.at[k], recv_sem=rsem.at[k_recv],
            device_id=dev, device_id_type=pl.DeviceIdType.MESH)
        copy.start()
        pending.append(copy)
        return copy

    def arrived(dst, k):
        pltpu.make_async_remote_copy(
            src_ref=dst, dst_ref=dst, send_sem=ssem.at[0], recv_sem=rsem.at[k],
            device_id=dev_e(0, 1 - c), device_id_type=pl.DeviceIdType.MESH).wait_recv()

    loads[0].wait()
    loads[1].wait()
    r0, r1 = route[0:1, :], route[1:2, :]
    line = lax.broadcasted_iota(jnp.int32, (16, tokens), 0)
    hit0, hit1 = line == r0, line == r1
    hits = jnp.where(hit0 | hit1, 1.0, 0.0)
    later = jnp.where(
        lax.broadcasted_iota(jnp.int32, (tokens, tokens), 1)
        > lax.broadcasted_iota(jnp.int32, (tokens, tokens), 0), 1.0, 0.0)
    rank = jnp.dot(hits.astype(BF), later.astype(BF), preferred_element_type=F32)
    slots[...] = jnp.where(hit0 | hit1, rank, NONE)
    table[...] = jnp.zeros_like(table)
    for n, (hit, r) in enumerate(((hit0, r0), (hit1, r1))):
        place = jnp.sum(jnp.where(hit, rank, 0.0), axis=0, keepdims=True) + r.astype(F32) * float(CAP)
        table[n:n + 1, :] = place
        table[n + 2:n + 3, :] = gates[n:n + 1, :]

    def picked(j):
        line = lax.broadcasted_iota(jnp.int32, (ROWS, tokens), 0).astype(F32)
        first = slots[pl.ds(chip(j) * 2, 1), :]
        second = slots[pl.ds(chip(j) * 2 + 1, 1), :] + float(CAP)
        chosen = jnp.where((line == first) | (line == second), 1.0, 0.0).astype(BF)
        got = jnp.dot(chosen, tok[...], preferred_element_type=F32).astype(BF)
        pick[j] = got.reshape(2, CAP, width)

    ks_d = {j: take(2) for j in (1, 3)}
    k_far = take(2)
    k_spread = take(4)
    k_own = take()
    za, zb = lax.rem(z, RING), lax.div(z, RING)

    loads[2].wait()
    line = lax.broadcasted_iota(jnp.int32, (2 * QUARTER, tokens), 0)
    slot = jnp.where(line < QUARTER, line, line - QUARTER) + za * QUARTER
    place = jnp.where(line < QUARTER, slots[pl.ds(chip(2) * 2, 1), :], slots[pl.ds(chip(2) * 2 + 1, 1), :])
    chosen = jnp.where(slot.astype(F32) == place, 1.0, 0.0).astype(BF)
    got = jnp.dot(chosen, tok[...], preferred_element_type=F32).astype(BF)
    farpick[...] = got.reshape(2, QUARTER, width)
    for j in (3, 1, 0):
        picked(j)
    pl.semaphore_wait(barrier, len(peers))
    for core in (0, 1):
        send(farpick.at[core], far_rows.at[za, c], dev_e(2, core), k_far + core, k_far + c)
    for j in (3, 1):
        for core in (0, 1):
            send(pick.at[j, core], rows.at[RING - j, c], dev_e(j, core), ks_d[j] + core, ks_d[j] + c)
    send(pick.at[0, 1 - c], rows.at[0, c], dev_e(0, 1 - c), k_own, k_own)
    rows[0, c] = pick[0, c]

    def vouch(n, hops):
        for j in (hops, -hops):
            pl.semaphore_signal(ready.at[n], inc=1, device_id=dev_z(j), device_id_type=pl.DeviceIdType.MESH)

    vouch(0, 2)

    def far_spread():
        for core in (0, 1):
            arrived(far_rows.at[za, core], k_far + core)
        for n, j in enumerate((1, -1)):
            send(far_rows.at[za], far_rows.at[za], dev_z(j), k_spread + n, k_spread + n)
        for n, j in enumerate((2, -2)):
            send(far_rows.at[za, n], far_rows.at[za, n], dev_z(j), k_spread + 2 + n, k_spread + 2 + n)

    def rows_here(j):
        if j == 0:
            arrived(rows.at[0, 1 - c], k_own)
        elif j == 2:
            arrived(far_rows.at[lax.rem(za + 3, RING)], k_spread)
            arrived(far_rows.at[lax.rem(za + 1, RING)], k_spread + 1)
            for n in (0, 1):
                arrived(far_rows.at[lax.rem(za + 2, RING), n], k_spread + 2 + n)
        else:
            for core in (0, 1):
                arrived(rows.at[j, core], ks_d[RING - j] + core)

    def rs_start(own, i, left, right, bufs):
        k = take(6)
        relay, done, _ = bufs
        opp, r, l = lax.rem(i + 2, RING), lax.rem(i + 1, RING), lax.rem(i + 3, RING)
        send(own[0].at[opp], relay[0], right, k, k)
        send(own[1].at[opp], relay[1], left, k + 1, k + 1)
        send(own[1].at[r], done[0], right, k + 2, k + 2)
        send(own[0].at[l], done[1], left, k + 3, k + 3)
        return k

    def rs_relay(k, own, i, left, right, bufs):
        relay, done, mixed = bufs
        r, l = lax.rem(i + 1, RING), lax.rem(i + 3, RING)
        arrived(relay[0], k)
        mixed[0][...] = (own[0][r].astype(F32) + relay[0][...].astype(F32)).astype(BF)
        send(mixed[0], done[2], right, k + 4, k + 4)
        arrived(relay[1], k + 1)
        mixed[1][...] = (own[1][l].astype(F32) + relay[1][...].astype(F32)).astype(BF)
        send(mixed[1], done[3], left, k + 5, k + 5)

    def rs_finish(k, own, i, bufs):
        done = bufs[1]
        for n in range(4):
            arrived(done[n], k + 2 + n)
        first = own[0][i].astype(F32) + done[1][...].astype(F32) + done[2][...].astype(F32)
        second = own[1][i].astype(F32) + done[0][...].astype(F32) + done[3][...].astype(F32)
        return first, second

    def rs_routed(own, i, left, right, across, bufs):
        k = take(6)
        relay, done, _ = bufs
        opp, r, l = lax.rem(i + 2, RING), lax.rem(i + 1, RING), lax.rem(i + 3, RING)
        send(own[0].at[opp], relay[0], across, k, k)
        send(own[1].at[opp], relay[1], across, k + 1, k + 1)
        send(own[1].at[r], done[0], right, k + 2, k + 2)
        send(own[0].at[l], done[1], left, k + 3, k + 3)
        send(own[0].at[r], done[2], right, k + 4, k + 4)
        send(own[1].at[l], done[3], left, k + 5, k + 5)
        return k

    def ag_start(at, i, left, right):
        k = take(6)
        send(at(0, i), at(0, i), right, k, k)
        send(at(1, i), at(1, i), left, k + 1, k + 1)
        send(at(1, i), at(1, i), right, k + 2, k + 2)
        send(at(0, i), at(0, i), left, k + 3, k + 3)
        return k

    def ag_routed(at, i, left, right, across):
        k = take(6)
        send(at(0, i), at(0, i), across, k + 4, k + 4)
        send(at(1, i), at(1, i), across, k + 5, k + 5)
        send(at(0, i), at(0, i), right, k, k)
        send(at(1, i), at(1, i), left, k + 1, k + 1)
        send(at(1, i), at(1, i), right, k + 2, k + 2)
        send(at(0, i), at(0, i), left, k + 3, k + 3)
        return k

    def ag_relay(k, at, i, left, right):
        r, l = lax.rem(i + 1, RING), lax.rem(i + 3, RING)
        arrived(at(0, l), k)
        send(at(0, l), at(0, l), right, k + 4, k + 4)
        arrived(at(1, r), k + 1)
        send(at(1, r), at(1, r), left, k + 5, k + 5)

    def ag_finish(k, at, i):
        opp, r, l = lax.rem(i + 2, RING), lax.rem(i + 1, RING), lax.rem(i + 3, RING)
        arrived(at(1, l), k + 2)
        arrived(at(0, r), k + 3)
        arrived(at(0, opp), k + 4)
        arrived(at(1, opp), k + 5)

    xl, xr, xo = dev_x(3), dev_x(1), dev_x(2)
    rs_k, ag_k = {}, {}

    def xbufs(j):
        return ([rl.at[j, h] for h in range(2)], [fin.at[j, n] for n in range(4)],
                [cmb.at[j, h] for h in range(2)])

    def xown(j):
        return [part.at[j, h] for h in range(2)]

    def hid_at(j):
        return lambda h, i: hid.at[j, h, i]

    def G(j):
        rows_here(j)
        if j == 0:
            loads[3].wait()
            loads[4].wait()
        here = (far_rows if j == 2 else rows.at[j])[...].reshape(ROWS, width)
        for n, w in enumerate((wg, wu)):
            got = jnp.dot(here, w[...], preferred_element_type=F32).astype(BF)
            part[j, n] = got.reshape(RING, PART, got.shape[1])
        if j in ROUTED_SUM:
            rs_k[j] = rs_routed(xown(j), x, xl, xr, xo, xbufs(j))
        else:
            rs_k[j] = rs_start(xown(j), x, xl, xr, xbufs(j))

    def R(j):
        if j not in ROUTED_SUM:
            rs_relay(rs_k[j], xown(j), x, xl, xr, xbufs(j))

    def H(j):
        gate, up = rs_finish(rs_k[j], xown(j), x, xbufs(j))
        if j in ROUTED_SUM:
            for n in range(2):
                arrived(rl.at[j, n], rs_k[j] + n)
            gate += rl[j, 0].astype(F32)
            up += rl[j, 1].astype(F32)
        got = (gate / (1.0 + jnp.exp(-gate)) * up).astype(BF)
        hw = got.shape[1] // 2
        hid[j, 0, x] = got[:, :hw]
        hid[j, 1, x] = got[:, hw:]
        if j in ROUTED_GATHER:
            ag_k[j] = ag_routed(hid_at(j), x, xl, xr, xo)
        else:
            ag_k[j] = ag_start(hid_at(j), x, xl, xr)

    def F(j):
        if j not in ROUTED_GATHER:
            ag_relay(ag_k[j], hid_at(j), x, xl, xr)

    k_ret = {j: take(2) for j in (1, 3)}
    k_rfar = take(4)
    cols = width // 2
    k_rown = take()

    def O(j, first_use=False):
        if j in ROUTED_GATHER:
            arrived(hid_at(j)(0, lax.rem(x + 3, RING)), ag_k[j])
            arrived(hid_at(j)(1, lax.rem(x + 1, RING)), ag_k[j] + 1)
        ag_finish(ag_k[j], hid_at(j), x)
        if first_use:
            loads[5].wait()
        hw = wd.shape[0] // 2
        got = jnp.dot(hid[j, 0].reshape(ROWS, hw), wd[0:hw], preferred_element_type=F32)
        got += jnp.dot(hid[j, 1].reshape(ROWS, hw), wd[hw:], preferred_element_type=F32)
        got = got.astype(BF)
        if j == 2:
            for q in (0, 1):
                far_out[q] = got[:, q * cols:(q + 1) * cols].reshape(far_out.shape[1:])
                for core in (0, 1):
                    send(far_out.at[q, :, core], far_ret.at[q, c], dev_e(2, core), k_rfar + 2 * q + core, k_rfar + 2 * q + c)
            return
        obuf[j] = got.reshape(2, CAP, width)
        if j == 0:
            send(obuf.at[0, 1 - c], ret.at[0, c], dev_e(0, 1 - c), k_rown, k_rown)
            ret[0, c] = obuf[0, c]
        else:
            for core in (0, 1):
                send(obuf.at[j, core], ret.at[RING - j, c], dev_e(j, core), k_ret[j] + core, k_ret[j] + c)

    def combine_table():
        by_token = table[...].T
        column = lax.broadcasted_iota(jnp.int32, (tokens, ROWS), 1)
        for j in range(RING):
            here = (column + chip(j) * ROWS).astype(F32)
            weight = jnp.where(here == by_token[:, 0:1], by_token[:, 2:3], 0.0)
            weight += jnp.where(here == by_token[:, 1:2], by_token[:, 3:4], 0.0)
            gm[j] = weight.astype(BF)

    def C(j, first=False):
        if j == 0:
            arrived(ret.at[0, 1 - c], k_rown)
        else:
            for core in (0, 1):
                arrived(ret.at[j, core], k_ret[RING - j] + core)
        got = jnp.dot(gm[j], ret[j].reshape(ROWS, width), preferred_element_type=F32)
        if first:
            acc[...] = got
        else:
            acc[...] += got

    G(0)
    combine_table()
    pl.semaphore_wait(ready.at[0], 2)
    vouch(1, 4)
    R(0)
    far_spread()
    H(0)
    G(1)
    G(3)
    F(0)
    R(1)
    R(3)
    G(2)
    O(0, True)
    H(1)
    R(2)
    H(3)
    F(1)
    F(3)
    H(2)
    O(1)
    O(3)
    C(0, True)
    F(2)
    O(2)
    C(1)
    C(3)

    block = tokens // RING
    sub = block // RING
    near_r, near_l, near_rr, near_ll = dev_z(1), dev_z(-1), dev_z(2), dev_z(-2)
    far_devs = (dev_z(4), dev_z(-4), dev_z(8))
    streams = [zbufs[6 * q:6 * q + 6] for q in range(2)]
    ks_near, ks_sum, ks_far, ks_out = [[take(n) for _ in range(2)] for n in (4, 3, 3, 3 * RING)]

    def ring(i, j):
        return lax.rem(i + RING + j, RING)

    for q, (mine, one, two, mid, far_in, done) in enumerate(streams):
        for core in (0, 1):
            arrived(far_ret.at[q, core], k_rfar + 2 * q + core)
        got = jnp.dot(gm[2], far_ret[q].reshape(ROWS, cols), preferred_element_type=F32)
        mine[...] = (acc[:, q * cols:(q + 1) * cols] + got).astype(BF).reshape(mine.shape)
        k = ks_near[q]
        send(mine.at[ring(za, 2), 0], two.at[0], near_rr, k + 2, k + 2)
        send(mine.at[ring(za, 2), 1], two.at[1], near_ll, k + 3, k + 3)
        send(mine.at[ring(za, 1)], one.at[0], near_r, k, k)
        send(mine.at[ring(za, -1)], one.at[1], near_l, k + 1, k + 1)
    pl.semaphore_wait(ready.at[1], 2)
    for q, (mine, one, two, mid, far_in, done) in enumerate(streams):
        k = ks_near[q]
        for n in (0, 1):
            arrived(two.at[n], k + 2 + n)
            arrived(one.at[n], k + n)
        total = mine[za].astype(F32) + one[0].astype(F32) + one[1].astype(F32) + two[...].astype(F32)
        mid[...] = total.astype(BF).reshape(mid.shape)
        for n in (2, 0, 1):
            send(mid.at[ring(zb, (1, -1, 2)[n])], far_in.at[n], far_devs[n], ks_sum[q] + n, ks_sum[q] + n)

    def spread(q, b):
        done = streams[q][5]
        k = ks_out[q] + 3 * b
        ref = done.at[za, b]
        send(ref, ref, near_r, k, k)
        send(ref, ref, near_l, k + 1, k + 1)
        send(ref, ref, dev_z(2 - 4 * lax.div(b, 2)), k + 2, k + 2)

    for q, (mine, one, two, mid, far_in, done) in enumerate(streams):
        for n in (0, 1, 2):
            arrived(far_in.at[n], ks_sum[q] + n)
        total = mid[zb].astype(F32) + far_in[0].astype(F32) + far_in[1].astype(F32) + far_in[2].astype(F32)
        done[za, zb] = total.astype(BF)
        for n in (2, 0, 1):
            send(done.at[za, zb], done.at[za, zb], far_devs[n], ks_far[q] + n, ks_far[q] + n)
        spread(q, zb)
    for n in (0, 1, 2):
        for q in range(2):
            b = ring(zb, (-1, 1, 2)[n])
            arrived(streams[q][5].at[za, b], ks_far[q] + n)
            spread(q, b)
    for q in range(2):
        done = streams[q][5]
        for b in range(RING):
            for n, j in enumerate((-1, 1, 2)):
                arrived(done.at[ring(za, j), b], ks_out[q] + 3 * b + n)
        out[:, q * cols:(q + 1) * cols] = done[...].reshape(tokens, cols)
    for copy in pending:
        copy.wait_send()


def local(tokens, route_ids, gates, w_gate, w_up, w_down):
    w_gate, w_up, w_down = w_gate[0], w_up[0], w_down[0]
    n, width = tokens.shape
    units = w_gate.shape[1]
    block = n // RING
    sub = block // RING
    V = pltpu.VMEM
    zbufs = []
    for _ in range(2):
        cols = width // 2
        zbufs += [V((RING, 2, block // 2, cols), BF), V((2, 2, block // 2, cols), BF),
                  V((2, block // 2, cols), BF), V((RING, sub, cols), BF),
                  V((3, sub, cols), BF), V((RING, RING, sub, cols), BF)]
    scratch = [
        V((2, n), jnp.int32), V((2, n), F32),
        V(tokens.shape, BF), V(w_gate.shape, BF), V(w_up.shape, BF), V(w_down.shape, BF),
        V((16, n), F32),
        V((128, n), F32),
        V((RING, 2, CAP, width), BF),
        V((RING, 2, CAP, width), BF),
        V((2, QUARTER, width), BF),
        V((RING, 2, QUARTER, width), BF),
        V((RING, 2, RING, PART, units), BF),
        V((RING, 2, PART, units), BF),
        V((RING, 4, PART, units), BF),
        V((RING, 2, PART, units), BF),
        V((RING, 2, RING, PART, units // 2), BF),
        V((RING, 2, CAP, width), BF),
        V((2, RING, 2, QUARTER, width // 2), BF),
        V((RING, 2, CAP, width), BF),
        V((2, 2, RING, QUARTER, width // 2), BF),
        V((RING, n, ROWS), BF),
        V((n, width), F32),
        *zbufs,
        pltpu.SemaphoreType.DMA((6,)),
        pltpu.SemaphoreType.DMA((NSEM,)),
        pltpu.SemaphoreType.DMA((NSEM,)),
        pltpu.SemaphoreType.REGULAR((2,)),
    ]
    vmem = pl.BlockSpec(memory_space=pltpu.VMEM)
    hbm = pl.BlockSpec(memory_space=pltpu.HBM)
    return pl.pallas_call(
        kernel,
        out_shape=jax.ShapeDtypeStruct((n, width), BF),
        in_specs=[hbm] * 6,
        out_specs=vmem,
        scratch_shapes=scratch,
        compiler_params=pltpu.CompilerParams(
            collective_id=0, has_side_effects=True, vmem_limit_bytes=40 * 1024 * 1024),
        name="expert_layer",
    )(*[pltpu.with_memory_space_constraint(v, pltpu.HBM)
        for v in (tokens, route_ids.T, gates.T, w_gate, w_up, w_down)])


def solution(mesh):
    return jax.shard_map(
        local,
        mesh=mesh,
        in_specs=(
            P("expert", "dp"),
            P("expert", None),
            P("expert", None),
            P("expert", "dp", "tensor"),
            P("expert", "dp", "tensor"),
            P("expert", "tensor", "dp"),
        ),
        out_specs=P("expert", "dp"),
        check_vma=False,
    )
```
